128 devices in a mesh: span: 8 (over x, y_lo), tok: 16 (over z, y_hi, core).
Axes of the slice: x: 4, y: 4 (y_hi: 2, y_lo: 2; y = y_hi * 2 + y_lo), z: 4, core: 2. Of those that a mesh axis runs over, the one named last changes fastest.
Arguments:
- latents: bfloat16 [8, 1024, 3584], P('span', 'tok'), may hold values from -6 to 6
- levels: int32 [8], P('span'), may hold values from 0 to 14
- visible: int32 [8, 8], replicated, may hold values 0 or 1
- frame_counts: int32 [8], replicated, may hold values from 0 to 2
- modulation: float32 [16, 3, 3584], replicated, may hold values from -4 to 4
- w_qkv: bfloat16 [3584, 3, 4096], P(None, None, 'tok')
- qk_gain: float32 [2, 4096], P(None, 'tok'), may hold values from 0 to 5
- w_out: bfloat16 [4096, 3584], P('tok'), may hold values from -0.09375 to 0.09375
- w_head: bfloat16 [3584, 96], replicated, may hold values from -0.09375 to 0.09375
- conv_w: bfloat16 [3, 96, 384], replicated, may hold values from -0.375 to 0.375
Outputs:
- denoised: bfloat16 [8, 1024, 3584], P('span', 'tok')
- decoded: bfloat16 [8, 1024, 384], P('span', 'tok')
The draws below stay inside these ranges and needn't reach their ends.
All inputs are finite; a program needn't handle non-finite values.
Results may differ from the reference program's by a relative error of at most 0.015.
Values may be sent and summed in bfloat16 or wider, within the bound.
A program may use at most 128 MiB of HBM per device.

```python
import jax
import jax.numpy as jnp
from jax import lax

D = 3584
HEADS = 32
HD = 128
CV = 96
CH = 384
FRAMES = 8
LEVELS = 16
KEEP = 2
SPOTS = 8
TOK_DEV = 64
CT = 1024
CLIPS = 8
HEADS_DEV = 2
N_TOK = 16


def draw_w_qkv(key, part):
    base = jax.random.normal(key, (D, 3, HEADS * HD), jnp.float32)
    base = jnp.clip(base, -6.0, 6.0) * D ** (-0.5)
    return base.astype(jnp.bfloat16)


def draw_qk_gain(key, part):
    return jax.random.uniform(key, (2, HEADS * HD), jnp.float32, 0.6, 1.6)


def set_ends(drawn, key, low, top_value):
    dims = drawn.shape
    spot = [jax.random.randint(jax.random.fold_in(key, axis), (), 0, dims[axis]) for axis in range(len(dims))]
    drawn = drawn.at[tuple(spot)].set(low)
    longest = dims.index(max(dims))
    spot[longest] = (spot[longest] + 1) % dims[longest]
    return drawn.at[tuple(spot)].set(top_value)


def level_of(stream_key, shape, split, least, top_value):
    loudness = 1.0
    for axis_at, blocks in split:
        steps = jax.random.uniform(jax.random.fold_in(jax.random.fold_in(stream_key, 6), axis_at), (blocks,), jnp.float32, least / len(split), top_value / len(split))
        loudness = loudness * jnp.repeat(jnp.exp(steps), shape[axis_at] // blocks).reshape((-1,) + (1,) * (len(shape) - 1 - axis_at))
    return loudness


def centred(own_key, extent, scale, bound, split=(), kind=jnp.bfloat16):
    factor_of = level_of(own_key, extent, split, -0.22, 0.18) if split else 1.0
    entries = jax.random.normal(own_key, extent, jnp.float32) * scale * factor_of
    return jnp.minimum(jnp.maximum(entries, -bound), bound).astype(kind)


def setup_inputs(seed: int = 0) -> dict:
    splits = jax.random.split(jax.random.key(seed), 11)
    latents = centred(splits[0], (CLIPS, CT, D), 1.0, 6.0, ((0, 8), (1, 16)))
    levels = set_ends(jax.random.randint(splits[1], (CLIPS,), 0, LEVELS - 1), jax.random.fold_in(splits[1], 1), 0, (LEVELS - 1) - 1).astype(jnp.int32)
    visible = set_ends((jax.random.randint(splits[2], (CLIPS, CLIPS), 0, 4) < 3).astype(jnp.int32), jax.random.fold_in(splits[2], 1), 0, 1)
    frame_counts = set_ends(jax.random.randint(splits[3], (CLIPS,), 0, KEEP + 1), jax.random.fold_in(splits[3], 1), 0, KEEP).astype(jnp.int32)
    modulation = centred(splits[4], (LEVELS, 3, D), 1.0, 4.0, (), jnp.float32)
    w_qkv = draw_w_qkv(jax.random.fold_in(splits[10], 71), 0)
    qk_gain = draw_qk_gain(jax.random.fold_in(splits[10], 71), 0)
    w_out = centred(splits[7], (HEADS * HD, D), (HEADS * HD) ** -0.5, 0.09375, ((0, 16),))
    w_head = centred(splits[8], (D, CV), D ** -0.5, 0.09375)
    conv_w = centred(splits[9], (3, CV, CH), (3 * CV) ** -0.5, 0.375)
    return {"latents": latents, "levels": levels, "visible": visible, "frame_counts": frame_counts, "modulation": modulation, "w_qkv": w_qkv, "qk_gain": qk_gain, "w_out": w_out, "w_head": w_head, "conv_w": conv_w}


EPS = 1e-06
NEG = -1e+30

def modulate(rows, shift, scale):
    values = rows.astype(jnp.float32)
    centre = values - lax.optimization_barrier(jnp.mean(values, -1, keepdims=True))
    spread = lax.optimization_barrier(jnp.mean(centre * centre, -1, keepdims=True))
    return (centre * lax.rsqrt(spread + EPS) * (1.0 + scale) + shift).astype(jnp.bfloat16)

def qk_scale(tensor, gain):
    square = lax.optimization_barrier(jnp.mean(tensor * tensor, -1, keepdims=True))
    return (tensor * lax.rsqrt(square + EPS) * gain.reshape(tensor.shape[-2], tensor.shape[-1])).astype(jnp.bfloat16)

def reference(latents, levels, visible, frame_counts, modulation, w_qkv, qk_gain, w_out, w_head, conv_w):
    clip_ids = jnp.arange(CLIPS, dtype=jnp.int32)
    place = jnp.arange(CT, dtype=jnp.int32)
    frame_of = place % TOK_DEV // SPOTS
    key_ok = frame_of[None, :] < frame_counts[:, None]
    w_flat = w_qkv.reshape(D, 3 * HEADS * HD)
    w_groups = w_out.reshape(N_TOK, HEADS_DEV * HD, D)
    state = latents
    table = modulation[levels]
    modulated = modulate(state, table[:, 0][:, None, :], table[:, 1][:, None, :])
    proj = jnp.dot(modulated.reshape(CLIPS * CT, D), w_flat, preferred_element_type=jnp.float32)
    proj = proj.reshape(CLIPS * CT, 3, HEADS, HD)
    query = qk_scale(proj[:, 0], qk_gain[0]).reshape(CLIPS, CT, N_TOK, HEADS_DEV, HD)
    query = query.transpose(0, 2, 1, 3, 4)
    keys = qk_scale(proj[:, 1], qk_gain[1]).reshape(CLIPS * CT, N_TOK, HEADS_DEV, HD).transpose(1, 0, 2, 3)
    values = proj[:, 2].astype(jnp.bfloat16).reshape(CLIPS * CT, N_TOK, HEADS_DEV, HD).transpose(1, 0, 2, 3)

    def per_clip(item):
        query_c, clip, rows_c, gate_c = item
        earlier = (clip_ids < clip) & (visible[clip] == 1)
        usable = ((clip_ids == clip)[:, None] | earlier[:, None] & key_ok).reshape(CLIPS * CT)

        def per_group(group):
            query_g, keys_g, values_g, weight_g = group
            scores = jnp.einsum('qhd,khd->hqk', query_g.astype(jnp.float32), keys_g.astype(jnp.float32)) * HD ** (-0.5)
            scores = jnp.where(usable[None, None, :], scores, NEG)
            best = lax.optimization_barrier(jnp.max(scores, -1, keepdims=True))
            terms = jnp.where(usable[None, None, :], jnp.exp(scores - best), 0.0)
            total = lax.optimization_barrier(jnp.sum(terms, -1))
            rounded = lax.optimization_barrier(terms.astype(jnp.bfloat16)).astype(jnp.float32)
            acc = jnp.einsum('hqk,khd->hqd', rounded, values_g.astype(jnp.float32))
            attended = (acc / total[..., None]).transpose(1, 0, 2).reshape(CT, HEADS_DEV * HD).astype(jnp.bfloat16)
            return jnp.dot(attended, weight_g, preferred_element_type=jnp.float32).astype(jnp.bfloat16)
        parts = lax.map(per_group, (query_c, keys, values, w_groups))
        mixed = lax.optimization_barrier(jnp.sum(lax.optimization_barrier(parts).astype(jnp.float32), 0))
        return (rows_c.astype(jnp.float32) + gate_c * mixed).astype(jnp.bfloat16)
    state = lax.map(per_clip, (query, clip_ids, state, table[:, 2]))
    feats = jnp.dot(state.reshape(CLIPS * CT, D), w_head, preferred_element_type=jnp.float32).astype(jnp.bfloat16)
    feats = feats.reshape(CLIPS, N_TOK, FRAMES, SPOTS, CV).transpose(1, 0, 2, 3, 4).reshape(N_TOK, CLIPS * FRAMES, SPOTS, CV)
    length = CLIPS * FRAMES
    padded = jnp.concatenate([jnp.zeros((N_TOK, 2, SPOTS, CV), jnp.bfloat16), feats], 1)
    conv = jnp.zeros((N_TOK * length * SPOTS, CH), jnp.float32)
    for tap in range(3):
        window = padded[:, 2 - tap:2 - tap + length].reshape(N_TOK * length * SPOTS, CV)
        conv = conv + jnp.dot(window, conv_w[tap], preferred_element_type=jnp.float32)
    decoded = jax.nn.silu(conv).astype(jnp.bfloat16)
    decoded = decoded.reshape(N_TOK, CLIPS, FRAMES, SPOTS, CH).transpose(1, 0, 2, 3, 4).reshape(CLIPS, CT, CH)
    return (state, decoded)
```

```python
import jax
import jax.numpy as jnp
from jax import lax
from jax.experimental import pallas as pl
from jax.experimental.pallas import tpu as pltpu
from jax.sharding import PartitionSpec as P

HD = 128
FRAMES = 8
KEEP = 2
SPOTS = 8
TOK_DEV = 64
EPS = 1e-06
LOG2E = 1.4426950408889634

MESH = pl.DeviceIdType.MESH
F32 = jnp.float32
BF16 = jnp.bfloat16

OWN, DOWN, UP, FAR, ACROSS, XDOWN, XUP, XFAR = range(8)
HALF = TOK_DEV // 2


def places():
    s = lax.axis_index("span")
    t = lax.axis_index("tok")
    z, yh, c = t // 4, (t // 2) % 2, t % 2
    x, yl = s // 2, s % 2

    def tok(z, yh, c):
        return z * 4 + yh * 2 + c

    return dict(
        s=s,
        up=(s, tok((z + 1) % 4, yh, c)),
        down=(s, tok((z + 3) % 4, yh, c)),
        across=(s, tok(z, 1 - yh, c)),
        twin=(s, tok(z, yh, 1 - c)),
        right=(((x + 1) % 4) * 2 + yl, t),
        left=(((x + 3) % 4) * 2 + yl, t),
        pair=(x * 2 + 1 - yl, t),
        after=((s + 1) % 8, t),
        before=((s + 7) % 8, t),
    )


def greet(at, names):
    barrier = pltpu.get_barrier_semaphore()
    for name in names:
        pl.semaphore_signal(barrier, inc=1, device_id=at[name], device_id_type=MESH)
    return lambda: pl.semaphore_wait(barrier, len(names))


class Post:
    def __init__(self, send, recv):
        self.send, self.recv, self.copies = send, recv, []

    def __call__(self, src, dst, device):
        index = len(self.copies)
        copy = pltpu.make_async_remote_copy(
            src_ref=src,
            dst_ref=dst,
            send_sem=self.send.at[index],
            recv_sem=self.recv.at[index],
            device_id=device,
            device_id_type=MESH,
        )
        copy.start()
        self.copies.append(copy)
        return copy

    def drain(self):
        for copy in self.copies:
            copy.wait_send()


GATHER_COPIES = 30 + 42 + 1
GROUPS = ((0, 128), (128, 256), (384, 256), (640, 256), (896, 128))


def gather_kernel(
    levels, lat, mod, wqkv, gain, wout,
    q_out, k_out, v_out, kv_out, wtwin,
    xbuf, wbuf, kvbuf, send, recv, local,
):
    at = places()
    peers = ("twin", "up", "down", "across", "right", "left", "pair")
    met = greet(at, peers)
    loads = [pltpu.make_async_copy(wqkv.at[j], wbuf.at[j], local.at[j]) for j in range(3)]
    for load in loads:
        load.start()
    level = levels[0]
    shift = mod[0, pl.ds(level, 1), :]
    scale = 1.0 + mod[1, pl.ds(level, 1), :]
    for row in range(0, TOK_DEV, 16):
        values = lat[row : row + 16, :].astype(F32)
        centre = values - jnp.mean(values, -1, keepdims=True)
        spread = jnp.mean(centre * centre, -1, keepdims=True)
        xbuf[row : row + 16, :] = (centre * lax.rsqrt(spread + EPS) * scale + shift).astype(BF16)
    met()
    post = Post(send, recv)

    def part(place, core, half):
        return xbuf.at[pl.ds((place * 2 + core) * TOK_DEV + half * HALF, HALF)]

    def hand(place, half, core=1):
        return post(part(place, 0, half), part(place, core, half), at["twin"])

    def move(source, target, half, to):
        return post(part(source, 0, half), part(target, 0, half), at[to])

    up, down, across, twin = {}, {}, {}, {}
    for first in (0, 1):
        up[first] = move(OWN, DOWN, first, "up")
        down[1 - first] = move(OWN, UP, 1 - first, "down")
        across[first] = move(OWN, ACROSS, first, "across")
        twin[OWN, first] = hand(OWN, first)
    weights = post(wout, wtwin, at["twin"])

    def project(group):
        start, rows = GROUPS[group]
        tiles = rows // TOK_DEV
        x = xbuf[start : start + rows, :]
        for j, out in enumerate((q_out, k_out, v_out)):
            p = jnp.dot(x, wbuf[j], preferred_element_type=F32)
            if j < 2:
                heads = []
                for h in range(2):
                    t = p[:, h * HD : (h + 1) * HD]
                    square = jnp.mean(t * t, -1, keepdims=True)
                    g = gain[j : j + 1, h * HD : (h + 1) * HD]
                    if j == 0:
                        g = g * (LOG2E * HD ** (-0.5))
                    heads.append(t * lax.rsqrt(square + EPS) * g)
                p = jnp.concatenate(heads, -1)
            out[start : start + rows, :] = p.astype(BF16)
            if j > 0:
                lead = p.reshape(tiles, FRAMES, SPOTS, 2 * HD)
                for f in range(KEEP):
                    kvbuf[0, f, start // 8 : (start + rows) // 8, (j - 1) * 256 : j * 256] = (
                        lead[:, f].reshape(tiles * SPOTS, 2 * HD).astype(BF16)
                    )

    ranges = ((0, 80), (80, 32), (112, 16))

    class Spread:
        def __init__(self, index):
            self.first, self.rows = ranges[index]

        def move(self, source, target, f, to):
            rows = pl.ds(self.first, self.rows)
            return post(kvbuf.at[source, f, rows], kvbuf.at[target, f, rows], at[to])

        def begin(self):
            self.right = [self.move(0, 1, f, "right") for f in range(2)]
            self.left = [self.move(0, 3, f, "left") for f in range(2)]
            self.pair = [self.move(0, 4, f, "pair") for f in range(2)]

        def second(self):
            self.right[0].wait_recv()
            self.far = [self.move(1, 2, 0, "right")]
            self.left[1].wait_recv()
            self.far.append(self.move(3, 2, 1, "left"))
            self.over_right, self.over_left = [], []
            for f in range(2):
                self.pair[f].wait_recv()
                self.over_right.append(self.move(4, 5, f, "right"))
                self.over_left.append(self.move(4, 7, f, "left"))
            self.right[1].wait_recv()
            self.left[0].wait_recv()

        def third(self):
            self.over_right[0].wait_recv()
            self.far.append(self.move(5, 6, 0, "right"))
            self.over_left[1].wait_recv()
            self.far.append(self.move(7, 6, 1, "left"))
            self.over_right[1].wait_recv()
            self.over_left[0].wait_recv()

        def end(self):
            for copy in self.far:
                copy.wait_recv()

    spread = [Spread(index) for index in range(3)]

    for half in range(2):
        twin[OWN, half].wait_recv()
    for load in loads:
        load.wait()
    project(0)

    far, over_up, over_down, over_far = {}, {}, {}, {}
    up[0].wait_recv()
    far[0] = move(DOWN, FAR, 0, "up")
    twin[DOWN, 0] = hand(DOWN, 0)
    down[1].wait_recv()
    far[1] = move(UP, FAR, 1, "down")
    twin[UP, 1] = hand(UP, 1)
    up[1].wait_recv()
    twin[DOWN, 1] = hand(DOWN, 1)
    down[0].wait_recv()
    twin[UP, 0] = hand(UP, 0)
    across[0].wait_recv()
    over_up[0] = move(ACROSS, XDOWN, 0, "up")
    over_down[0] = move(ACROSS, XUP, 0, "down")
    twin[ACROSS, 0] = hand(ACROSS, 0)
    for place in (DOWN, UP):
        for half in range(2):
            twin[place, half].wait_recv()
    project(1)

    for half in range(2):
        far[half].wait_recv()
        twin[FAR, half] = hand(FAR, half)
    across[1].wait_recv()
    over_up[1] = move(ACROSS, XDOWN, 1, "up")
    over_down[1] = move(ACROSS, XUP, 1, "down")
    twin[ACROSS, 1] = hand(ACROSS, 1)
    for place in (FAR, ACROSS):
        for half in range(2):
            twin[place, half].wait_recv()
    project(2)
    spread[0].begin()

    over_up[0].wait_recv()
    over_far[0] = move(XDOWN, XFAR, 0, "up")
    twin[XDOWN, 0] = hand(XDOWN, 0)
    over_down[0].wait_recv()
    twin[XUP, 0] = hand(XUP, 0)
    over_down[1].wait_recv()
    over_far[1] = move(XUP, XFAR, 1, "down")
    twin[XUP, 1] = hand(XUP, 1)
    over_up[1].wait_recv()
    twin[XDOWN, 1] = hand(XDOWN, 1)
    spread[0].second()
    for place in (XDOWN, XUP):
        for half in range(2):
            twin[place, half].wait_recv()
    project(3)
    spread[1].begin()

    for half in range(2):
        over_far[half].wait_recv()
        twin[XFAR, half] = hand(XFAR, half)
    spread[0].third()
    for half in range(2):
        twin[XFAR, half].wait_recv()
    project(4)
    spread[2].begin()
    spread[1].second()
    spread[2].second()
    spread[1].third()
    spread[2].third()
    for item in spread:
        item.end()
    keep = pltpu.make_async_copy(kvbuf.at[pl.ds(1, 7)], kv_out, local.at[3])
    keep.start()
    weights.wait_recv()
    post.drain()
    keep.wait()
    assert len(post.copies) == GATHER_COPIES


def gather(levels, lat, mod, wqkv, gain, wout):
    rows, width = 16 * TOK_DEV, lat.shape[1]
    vmem = pl.BlockSpec(memory_space=pltpu.VMEM)
    anywhere = pl.BlockSpec(memory_space=pl.ANY)
    tensor = jax.ShapeDtypeStruct((rows, 2 * HD), BF16)
    return pl.pallas_call(
        gather_kernel,
        out_shape=(
            tensor, tensor, tensor,
            jax.ShapeDtypeStruct((7, KEEP, 128, 512), BF16),
            jax.ShapeDtypeStruct(wout.shape, BF16),
        ),
        in_specs=[pl.BlockSpec(memory_space=pltpu.SMEM), vmem, vmem, anywhere, vmem, anywhere],
        out_specs=(vmem, vmem, vmem, anywhere, anywhere),
        scratch_shapes=[
            pltpu.VMEM((rows, width), BF16),
            pltpu.VMEM((3, width, 2 * HD), BF16),
            pltpu.VMEM((8, KEEP, 128, 512), BF16),
            pltpu.SemaphoreType.DMA((GATHER_COPIES,)),
            pltpu.SemaphoreType.DMA((GATHER_COPIES,)),
            pltpu.SemaphoreType.DMA((4,)),
        ],
        compiler_params=pltpu.CompilerParams(
            collective_id=0, has_side_effects=True, vmem_limit_bytes=44 * 2**20
        ),
        name="gather_project",
    )(levels, lat, mod, wqkv, gain, wout)


def attend_kernel(visible, counts, q, k, v, kv, out, best, total, acc):
    s = lax.axis_index("span")
    x, yl = s // 2, s % 2
    contract = (((1,), (1,)), ((), ()))
    for h in range(2):
        cols = slice(h * HD, (h + 1) * HD)
        scores = lax.dot_general(q[:, cols], k[:, cols], contract, preferred_element_type=F32)
        top = jnp.max(scores, -1, keepdims=True)
        terms = jnp.exp2(scores - top)
        best[h] = top
        total[h] = jnp.sum(terms, -1, keepdims=True)
        acc[h] = jnp.dot(terms.astype(BF16), v[:, cols], preferred_element_type=F32)

    def fold(keys, values):
        for h in range(2):
            cols = slice(h * HD, (h + 1) * HD)
            scores = lax.dot_general(
                q[:, cols], keys[:, cols], contract, preferred_element_type=F32
            )
            old = best[h]
            fresh = jnp.maximum(old, jnp.max(scores, -1, keepdims=True))
            terms = jnp.exp2(scores - fresh)
            decay = jnp.exp2(old - fresh)
            best[h] = fresh
            total[h] = total[h] * decay + jnp.sum(terms, -1, keepdims=True)
            acc[h] = acc[h] * decay + jnp.dot(
                terms.astype(BF16), values[:, cols], preferred_element_type=F32
            )

    def one(index, carry):
        place = index + 1
        source = ((x + 4 - place % 4) % 4) * 2 + (yl + place // 4) % 2
        seen = (source < s) & (visible[s, source] == 1)
        count = counts[source]

        @pl.when(seen & (count >= 2))
        def _():
            both = kv[index].reshape(2 * 128, 512)
            fold(both[:, :256], both[:, 256:])

        @pl.when(seen & (count == 1))
        def _():
            lead = kv[index, 0]
            fold(lead[:, :256], lead[:, 256:])

        return carry

    lax.fori_loop(0, 7, one, 0)
    for h in range(2):
        out[:, h * HD : (h + 1) * HD] = (acc[h] / total[h]).astype(BF16)


def attend(visible, counts, q, k, v, kv):
    rows = q.shape[0]
    block = 256
    smem = pl.BlockSpec(memory_space=pltpu.SMEM)
    whole = pl.BlockSpec((rows, 2 * HD), lambda i: (0, 0))
    tile = pl.BlockSpec((block, 2 * HD), lambda i: (i, 0))
    return pl.pallas_call(
        attend_kernel,
        grid=(rows // block,),
        out_shape=jax.ShapeDtypeStruct((rows, 2 * HD), BF16),
        in_specs=[
            smem, smem, tile, whole, whole,
            pl.BlockSpec((7, KEEP, 128, 512), lambda i: (0, 0, 0, 0)),
        ],
        out_specs=tile,
        scratch_shapes=[
            pltpu.VMEM((2, block, 1), F32),
            pltpu.VMEM((2, block, 1), F32),
            pltpu.VMEM((2, block, HD), F32),
        ],
        compiler_params=pltpu.CompilerParams(vmem_limit_bytes=40 * 2**20),
        name="attend",
    )(visible, counts, q, k, v, kv)


REDUCE_COPIES = 16


def reduce_kernel(
    levels, att, wout, wtwin, lat, mod, whead, conv_w,
    den, dec,
    wbuf, atwin, partial, outbox, farbox, zbox, ybox, heads, taps, tail, halo,
    send, recv, local,
):
    at = places()
    peers = ("twin", "up", "down", "across", "after", "before")
    met = greet(at, peers)
    width = lat.shape[1]
    depth = wout.shape[0]
    loads = [
        pltpu.make_async_copy(wout, wbuf.at[pl.ds(0, depth)], local.at[0]),
        pltpu.make_async_copy(wtwin, wbuf.at[pl.ds(depth, depth)], local.at[1]),
    ]
    for load in loads:
        load.start()
    met()
    post = Post(send, recv)
    shared = post(att.at[:, 1], atwin, at["twin"])
    heads[96:, :] = jnp.zeros((32, width), BF16)
    heads[:96, :] = whead[...]
    taps[:, 96:, :] = jnp.zeros((3, 32, taps.shape[2]), BF16)
    taps[:, :96, :] = conv_w[...]
    for load in loads:
        load.wait()
    shared.wait_recv()
    tile = 512

    def multiply(spots):
        a = jnp.concatenate(
            [jnp.concatenate([att[p, 0], atwin[p]], -1) for p in spots], 0
        )
        for col in range(0, width, tile):
            r = jnp.dot(a, wbuf[:, col : col + tile], preferred_element_type=F32)
            for i, p in enumerate(spots):
                partial[p, :, col : col + tile] = r[i * TOK_DEV : (i + 1) * TOK_DEV]

    def rows(half):
        return slice(half * HALF, (half + 1) * HALF)

    def ship(spot, half, box, to, *added):
        value = partial[spot, rows(half), :]
        for other in added:
            value = value + other[rows(half), :].astype(F32)
        outbox[spot, rows(half), :] = value.astype(BF16)
        piece = pl.ds(half * HALF, HALF)
        return post(outbox.at[spot, piece], box.at[piece], at[to])


    multiply((XFAR,))
    far_up = ship(XFAR, 0, farbox.at[1], "up")
    far_down = ship(XFAR, 1, farbox.at[1], "down")
    multiply((XDOWN, XUP))
    down, up = {}, {}
    down[1, 0] = ship(XDOWN, 0, zbox.at[1, 1], "down")
    multiply((FAR,))
    far_up.wait_recv()
    up[1, 0] = ship(XUP, 0, zbox.at[1, 0], "up", farbox.at[1])
    up[1, 1] = ship(XUP, 1, zbox.at[1, 0], "up")
    far_down.wait_recv()
    down[1, 1] = ship(XDOWN, 1, zbox.at[1, 1], "down", farbox.at[1])
    far_up = ship(FAR, 0, farbox.at[0], "up")
    far_down = ship(FAR, 1, farbox.at[0], "down")
    multiply((DOWN, UP))
    up[0, 1] = ship(UP, 1, zbox.at[0, 0], "up")
    down[0, 0] = ship(DOWN, 0, zbox.at[0, 1], "down")
    multiply((ACROSS, OWN))
    over = {}
    for half in range(2):
        up[1, half].wait_recv()
        down[1, half].wait_recv()
        over[half] = ship(ACROSS, half, ybox, "across", zbox.at[1, 0], zbox.at[1, 1])
    far_up.wait_recv()
    up[0, 0] = ship(UP, 0, zbox.at[0, 0], "up", farbox.at[0])
    far_down.wait_recv()
    down[0, 1] = ship(DOWN, 1, zbox.at[0, 1], "down", farbox.at[0])

    gate = mod[2, pl.ds(levels[0], 1), :]
    for half in (1, 0):
        up[0, half].wait_recv()
        down[0, half].wait_recv()
        if half == 1:
            continue
        over[0].wait_recv()
        over[1].wait_recv()
    for row in range(0, TOK_DEV, 16):
        piece = slice(row, row + 16)
        mixed = partial[OWN, piece, :]
        for box in (zbox.at[0, 0], zbox.at[0, 1], ybox):
            mixed = mixed + box[piece, :].astype(F32)
        den[piece, :] = (lat[piece, :].astype(F32) + gate * mixed).astype(BF16)
    feats = lax.dot_general(
        den[...], heads[...], (((1,), (1,)), ((), ())), preferred_element_type=F32
    ).astype(BF16).astype(F32)
    tail[...] = feats[TOK_DEV - 2 * SPOTS :].astype(BF16)
    edge = post(tail, halo, at["after"])
    edge.wait_recv()
    earlier = jnp.where(at["s"] > 0, halo[...].astype(F32), 0.0)
    sequence = jnp.concatenate([earlier, feats], 0)
    conv = jnp.zeros(dec.shape, F32)
    for tap in range(3):
        begin = (2 - tap) * SPOTS
        window = sequence[begin : begin + TOK_DEV].astype(BF16)
        conv = conv + jnp.dot(window, taps[tap], preferred_element_type=F32)
    dec[...] = (conv / (1.0 + jnp.exp(-conv))).astype(BF16)
    post.drain()
    assert len(post.copies) == REDUCE_COPIES


def reduce(levels, att, wout, wtwin, lat, mod, whead, conv_w):
    width, depth = lat.shape[1], wout.shape[0]
    vmem = pl.BlockSpec(memory_space=pltpu.VMEM)
    anywhere = pl.BlockSpec(memory_space=pl.ANY)
    return pl.pallas_call(
        reduce_kernel,
        out_shape=(
            jax.ShapeDtypeStruct(lat.shape, BF16),
            jax.ShapeDtypeStruct((lat.shape[0], conv_w.shape[2]), BF16),
        ),
        in_specs=[
            pl.BlockSpec(memory_space=pltpu.SMEM), vmem, anywhere, anywhere, vmem, vmem, vmem, vmem,
        ],
        out_specs=(vmem, vmem),
        scratch_shapes=[
            pltpu.VMEM((2 * depth, width), BF16),
            pltpu.VMEM((8, TOK_DEV, 2 * HD), BF16),
            pltpu.VMEM((8, TOK_DEV, width), F32),
            pltpu.VMEM((8, TOK_DEV, width), BF16),
            pltpu.VMEM((2, TOK_DEV, width), BF16),
            pltpu.VMEM((2, 2, TOK_DEV, width), BF16),
            pltpu.VMEM((TOK_DEV, width), BF16),
            pltpu.VMEM((128, width), BF16),
            pltpu.VMEM((3, 128, conv_w.shape[2]), BF16),
            pltpu.VMEM((2 * SPOTS, 128), BF16),
            pltpu.VMEM((2 * SPOTS, 128), BF16),
            pltpu.SemaphoreType.DMA((REDUCE_COPIES,)),
            pltpu.SemaphoreType.DMA((REDUCE_COPIES,)),
            pltpu.SemaphoreType.DMA((2,)),
        ],
        compiler_params=pltpu.CompilerParams(
            collective_id=1, has_side_effects=True, vmem_limit_bytes=44 * 2**20
        ),
        name="reduce_decode",
    )(levels, att, wout, wtwin, lat, mod, whead, conv_w)


def per_device(
    latents, levels, visible, frame_counts, modulation, w_qkv, qk_gain, w_out, w_head, conv_w
):
    lat = latents[0]
    mod = modulation.transpose(1, 0, 2)
    query, keys, values, lead, wtwin = gather(
        levels, lat, mod, w_qkv.transpose(1, 0, 2), qk_gain, w_out
    )
    attended = attend(visible, frame_counts, query, keys, values, lead)
    attended = attended.reshape(8, 2, TOK_DEV, 2 * HD)
    denoised, decoded = reduce(levels, attended, w_out, wtwin, lat, mod, w_head.T, conv_w)
    return (denoised[None], decoded[None])


def solution(mesh):
    placed = (
        P("span", "tok", None),
        P("span"),
        P(),
        P(),
        P(),
        P(None, None, "tok"),
        P(None, "tok"),
        P("tok", None),
        P(),
        P(),
    )
    return jax.shard_map(
        per_device,
        mesh=mesh,
        in_specs=placed,
        out_specs=(P("span", "tok", None), P("span", "tok", None)),
        check_vma=False,
    )
```

```python
import jax
import jax.numpy as jnp
from jax import lax
from jax.experimental import pallas as pl
from jax.experimental.pallas import tpu as pltpu
from jax.sharding import PartitionSpec as P

HD = 128
FRAMES = 8
KEEP = 2
SPOTS = 8
TOK_DEV = 64
EPS = 1e-06
LOG2E = 1.4426950408889634

MESH = pl.DeviceIdType.MESH
F32 = jnp.float32
BF16 = jnp.bfloat16

OWN, DOWN, UP, FAR, ACROSS, XDOWN, XUP, XFAR = range(8)
HALF = TOK_DEV // 2


def places():
    s = lax.axis_index("span")
    t = lax.axis_index("tok")
    z, yh, c = t // 4, (t // 2) % 2, t % 2
    x, yl = s // 2, s % 2

    def tok(z, yh, c):
        return z * 4 + yh * 2 + c

    return dict(
        s=s,
        up=(s, tok((z + 1) % 4, yh, c)),
        down=(s, tok((z + 3) % 4, yh, c)),
        across=(s, tok(z, 1 - yh, c)),
        twin=(s, tok(z, yh, 1 - c)),
        right=(((x + 1) % 4) * 2 + yl, t),
        left=(((x + 3) % 4) * 2 + yl, t),
        pair=(x * 2 + 1 - yl, t),
        after=((s + 1) % 8, t),
        before=((s + 7) % 8, t),
    )


def greet(at, names):
    barrier = pltpu.get_barrier_semaphore()
    for name in names:
        pl.semaphore_signal(barrier, inc=1, device_id=at[name], device_id_type=MESH)
    return lambda: pl.semaphore_wait(barrier, len(names))


class Post:
    def __init__(self, send, recv):
        self.send, self.recv, self.copies = send, recv, []

    def __call__(self, src, dst, device):
        index = len(self.copies)
        copy = pltpu.make_async_remote_copy(
            src_ref=src,
            dst_ref=dst,
            send_sem=self.send.at[index],
            recv_sem=self.recv.at[index],
            device_id=device,
            device_id_type=MESH,
        )
        copy.start()
        self.copies.append(copy)
        return copy

    def drain(self):
        for copy in self.copies:
            copy.wait_send()

COPIES = 30 + 56 + 1 + 8 + 14 + 1
GROUPS = ((0, 128), (128, 256), (384, 256), (640, 256), (896, 128))
PENALTY = 1e30
WIDE = 2 * HD


def layer_kernel(
    levels, visible, counts, lat_in, mod_in, wqkv, gain_in, wout, whead, conv_w,
    den, dec,
    lat, mod, gain, xbuf, wbuf, qbuf, kbuf, vbuf, kvbuf, best, total, acc, att, atwin,
    obuf, partial, outbox, fx, cx, fo, yx, zd, zu, ya, heads, taps, tail, halo,
    send, recv, local,
):
    at = places()
    s = at["s"]
    peers = ("twin", "up", "down", "across", "right", "left", "pair", "after", "before")
    met = greet(at, peers)
    width, depth = lat.shape[1], wout.shape[0]

    def load(index, source, target):
        copy = pltpu.make_async_copy(source, target, local.at[index])
        copy.start()
        return copy

    first_loads = [load(0, lat_in, lat), load(1, mod_in, mod), load(2, gain_in, gain)]
    weights = [load(3 + j, wqkv.at[j], wbuf.at[j]) for j in range(3)]
    late_loads = [
        load(6, wout, obuf.at[pl.ds(0, depth)]),
        load(7, whead, heads.at[pl.ds(0, 96)]),
        load(8, conv_w, taps.at[:, pl.ds(0, 96)]),
    ]
    for item in first_loads:
        item.wait()
    level = levels[0]
    shift = mod[0, pl.ds(level, 1), :]
    scale = 1.0 + mod[1, pl.ds(level, 1), :]
    for row in range(0, TOK_DEV, 16):
        values = lat[row : row + 16, :].astype(F32)
        centre = values - jnp.mean(values, -1, keepdims=True)
        spread = jnp.mean(centre * centre, -1, keepdims=True)
        xbuf[row : row + 16, :] = (centre * lax.rsqrt(spread + EPS) * scale + shift).astype(BF16)
    met()
    post = Post(send, recv)

    def part(place, core, half):
        return xbuf.at[pl.ds((place * 2 + core) * TOK_DEV + half * HALF, HALF)]

    twin = {}

    def hand(place, half):
        twin[place, half] = post(part(place, 0, half), part(place, 1, half), at["twin"])

    def move(source, target, half, to):
        return post(part(source, 0, half), part(target, 0, half), at[to])

    def settle(*names):
        for place in names:
            for half in range(2):
                twin[place, half].wait_recv()

    up, down, across = {}, {}, {}
    for first in (0, 1):
        up[first] = move(OWN, DOWN, first, "up")
        down[1 - first] = move(OWN, UP, 1 - first, "down")
        across[first] = move(OWN, ACROSS, first, "across")
        hand(OWN, first)
    wtwin = post(wout, obuf.at[pl.ds(depth, depth)], at["twin"])

    def project(group):
        start, rows = GROUPS[group]
        tiles = rows // TOK_DEV
        x = xbuf[start : start + rows, :]
        for j, out in enumerate((qbuf, kbuf, vbuf)):
            p = jnp.dot(x, wbuf[j], preferred_element_type=F32)
            if j < 2:
                parts = []
                for h in range(2):
                    t = p[:, h * HD : (h + 1) * HD]
                    square = jnp.mean(t * t, -1, keepdims=True)
                    g = gain[j : j + 1, h * HD : (h + 1) * HD]
                    if j == 0:
                        g = g * (LOG2E * HD ** (-0.5))
                    parts.append(t * lax.rsqrt(square + EPS) * g)
                p = jnp.concatenate(parts, -1)
            out[start : start + rows, :] = p.astype(BF16)
            if j > 0:
                lead = p.reshape(tiles, FRAMES, SPOTS, WIDE)
                for f in range(KEEP):
                    kvbuf[0, f, start // 8 : (start + rows) // 8, (j - 1) * WIDE : j * WIDE] = (
                        lead[:, f].reshape(tiles * SPOTS, WIDE).astype(BF16)
                    )

    ranges = ((0, 48), (48, 32), (80, 32), (112, 16))

    class Spread:
        def __init__(self, index):
            self.first, self.rows = ranges[index]

        def move(self, source, target, f, to):
            rows = pl.ds(self.first, self.rows)
            return post(kvbuf.at[source, f, rows], kvbuf.at[target, f, rows], at[to])

        def begin(self):
            self.right = [self.move(0, 1, f, "right") for f in range(2)]
            self.left = [self.move(0, 3, f, "left") for f in (1, 0)][::-1]
            self.pair = [self.move(0, 4, f, "pair") for f in range(2)]

        def second(self):
            self.right[0].wait_recv()
            self.far = [self.move(1, 2, 0, "right")]
            self.left[1].wait_recv()
            self.far.append(self.move(3, 2, 1, "left"))
            self.over_right, self.over_left = [], []
            for f in range(2):
                self.pair[f].wait_recv()
                self.over_right.append(self.move(4, 5, f, "right"))
                self.over_left.append(self.move(4, 7, f, "left"))
            self.right[1].wait_recv()
            self.left[0].wait_recv()

        def third(self):
            self.over_right[0].wait_recv()
            self.far.append(self.move(5, 6, 0, "right"))
            self.over_left[1].wait_recv()
            self.far.append(self.move(7, 6, 1, "left"))
            self.over_right[1].wait_recv()
            self.over_left[0].wait_recv()

        def end(self):
            for copy in self.far:
                copy.wait_recv()

    spread = [Spread(index) for index in range(4)]

    settle(OWN)
    for item in weights:
        item.wait()
    project(0)

    far, over, cross_y, over_far = {}, {}, {}, {}
    up[0].wait_recv()
    far[0] = move(DOWN, FAR, 0, "up")
    cross_y[0] = move(DOWN, XDOWN, 0, "across")
    hand(DOWN, 0)
    down[1].wait_recv()
    far[1] = move(UP, FAR, 1, "down")
    cross_y[1] = move(UP, XUP, 1, "across")
    hand(UP, 1)
    across[0].wait_recv()
    over[0] = move(ACROSS, XUP, 0, "down")
    hand(ACROSS, 0)
    up[1].wait_recv()
    hand(DOWN, 1)
    down[0].wait_recv()
    hand(UP, 0)
    across[1].wait_recv()
    over[1] = move(ACROSS, XDOWN, 1, "up")
    hand(ACROSS, 1)
    settle(DOWN, UP)
    project(1)
    spread[0].begin()

    for half in range(2):
        far[half].wait_recv()
        hand(FAR, half)
    cross_y[0].wait_recv()
    over_far[0] = move(XDOWN, XFAR, 0, "up")
    hand(XDOWN, 0)
    settle(FAR, ACROSS)
    project(2)
    spread[1].begin()
    spread[0].second()

    cross_y[1].wait_recv()
    over_far[1] = move(XUP, XFAR, 1, "down")
    hand(XUP, 1)
    over[1].wait_recv()
    hand(XDOWN, 1)
    over[0].wait_recv()
    hand(XUP, 0)
    settle(XDOWN, XUP)
    project(3)
    spread[2].begin()
    spread[0].third()
    spread[1].second()

    for half in range(2):
        over_far[half].wait_recv()
        hand(XFAR, half)
    settle(XFAR)
    project(4)
    spread[3].begin()
    spread[1].third()
    spread[2].second()

    contract = (((1,), (1,)), ((), ()))
    x, yl = s // 2, s % 2
    penalties = []
    for place in range(1, 8):
        source = ((x + 4 - place % 4) % 4) * 2 + (yl + place // 4) % 2
        seen = (source < s) & (visible[s, source] == 1)
        count = counts[source]
        penalties.append(
            [jnp.where(seen & (f < count), 0.0, PENALTY).astype(F32) for f in range(KEEP)]
        )

    def queries(place):
        return pl.ds(place * 128, 128)

    def own_clip(place):
        rows = queries(place)
        for h in range(2):
            cols = slice(h * HD, (h + 1) * HD)
            scores = lax.dot_general(
                qbuf[rows, cols], kbuf[:, cols], contract, preferred_element_type=F32
            )
            top = jnp.max(scores, -1, keepdims=True)
            terms = jnp.exp2(scores - top)
            best[h, rows] = top
            total[h, rows] = jnp.sum(terms, -1, keepdims=True)
            acc[h, rows] = jnp.dot(
                terms.astype(BF16), vbuf[:, cols], preferred_element_type=F32
            )

    def earlier_clips(place):
        rows = queries(place)
        for h in range(2):
            cols = slice(h * HD, (h + 1) * HD)
            query = qbuf[rows, cols]
            old = best[h, rows]
            top = old
            scores = []
            for i in range(7):
                for f in range(KEEP):
                    piece = lax.dot_general(
                        query, kvbuf[i + 1, f, :, cols], contract, preferred_element_type=F32
                    )
                    scores.append(piece)
                    top = jnp.maximum(
                        top, jnp.max(piece, -1, keepdims=True) - penalties[i][f]
                    )
            decay = jnp.exp2(old - top)
            terms = [
                jnp.exp2(piece - (top + penalties[n // 2][n % 2]))
                for n, piece in enumerate(scores)
            ]
            plain = terms[0]
            for term in terms[1:]:
                plain = plain + term
            norm = total[h, rows] * decay + jnp.sum(plain, -1, keepdims=True)
            values = kvbuf[1:8, :, :, WIDE + h * HD : WIDE + (h + 1) * HD].reshape(7 * WIDE, HD)
            mixed = acc[h, rows] * decay + jnp.dot(
                jnp.concatenate([term.astype(BF16) for term in terms], -1),
                values,
                preferred_element_type=F32,
            )
            out = (mixed / norm).astype(BF16)
            att[place, 0, :, cols] = out[:TOK_DEV]
            att[place, 1, :, cols] = out[TOK_DEV:]

    shared = {}

    def swap(place):
        shared[place] = post(att.at[place, 1], atwin.at[place], at["twin"])

    tile = 512

    def multiply(*spots):
        for p in spots:
            shared[p].wait_recv()
        a = jnp.concatenate(
            [jnp.concatenate([att[p, 0], atwin[p]], -1) for p in spots], 0
        )
        for col in range(0, width, tile):
            r = jnp.dot(a, obuf[:, col : col + tile], preferred_element_type=F32)
            for i, p in enumerate(spots):
                partial[p, :, col : col + tile] = r[i * TOK_DEV : (i + 1) * TOK_DEV]

    def ship(spot, half, box, to, *added):
        rows = slice(half * HALF, (half + 1) * HALF)
        value = partial[spot, rows, :]
        for other in added:
            value = value + other[rows, :].astype(F32)
        outbox[spot, rows, :] = value.astype(BF16)
        piece = pl.ds(half * HALF, HALF)
        return post(outbox.at[spot, piece], box.at[piece], at[to])

    own_clip(XFAR)
    spread[2].third()
    spread[3].second()
    own_clip(XDOWN)
    spread[3].third()
    own_clip(XUP)
    for item in spread:
        item.end()
    earlier_clips(XFAR)
    swap(XFAR)
    for item in late_loads:
        item.wait()
    wtwin.wait_recv()
    heads[96:, :] = jnp.zeros((32, width), BF16)
    taps[:, 96:, :] = jnp.zeros((3, 32, taps.shape[2]), BF16)
    multiply(XFAR)
    fx0 = ship(XFAR, 0, fx, "up")
    fx1 = ship(XFAR, 1, fx, "down")

    earlier_clips(XDOWN)
    swap(XDOWN)
    earlier_clips(XUP)
    swap(XUP)
    own_clip(FAR)
    multiply(XDOWN, XUP)
    cx1 = ship(XUP, 1, cx, "up")
    cx0 = ship(XDOWN, 0, cx, "down")
    earlier_clips(FAR)
    swap(FAR)
    fx0.wait_recv()
    yx0 = ship(XUP, 0, yx, "across", fx)
    fx1.wait_recv()
    yx1 = ship(XDOWN, 1, yx, "across", fx)
    multiply(FAR)
    fo0 = ship(FAR, 0, fo, "up")
    fo1 = ship(FAR, 1, fo, "down")

    def rest(index, carry):
        own_clip(index)
        earlier_clips(index)
        return carry

    lax.fori_loop(DOWN, UP + 1, rest, 0)
    swap(DOWN)
    swap(UP)
    own_clip(ACROSS)
    multiply(DOWN, UP)
    zd1 = ship(UP, 1, zd, "up")
    zu0 = ship(DOWN, 0, zu, "down")
    earlier_clips(ACROSS)
    swap(ACROSS)
    own_clip(OWN)
    multiply(ACROSS)
    cx1.wait_recv()
    ya1 = ship(ACROSS, 1, ya, "across", cx)
    cx0.wait_recv()
    ya0 = ship(ACROSS, 0, ya, "across", cx)
    fo0.wait_recv()
    yx0.wait_recv()
    zd0 = ship(UP, 0, zd, "up", fo, yx)
    fo1.wait_recv()
    yx1.wait_recv()
    zu1 = ship(DOWN, 1, zu, "down", fo, yx)
    earlier_clips(OWN)
    swap(OWN)
    multiply(OWN)

    gate = mod[2, pl.ds(level, 1), :]
    for copy in (zd1, zu0, ya1, zd0, zu1, ya0):
        copy.wait_recv()
    for row in range(0, TOK_DEV, 16):
        piece = slice(row, row + 16)
        mixed = partial[OWN, piece, :]
        for box in (zd, zu, ya):
            mixed = mixed + box[piece, :].astype(F32)
        den[piece, :] = (lat[piece, :].astype(F32) + gate * mixed).astype(BF16)
    feats = lax.dot_general(
        den[...], heads[...], contract, preferred_element_type=F32
    ).astype(BF16).astype(F32)
    tail[...] = feats[TOK_DEV - 2 * SPOTS :].astype(BF16)
    edge = post(tail, halo, at["after"])
    edge.wait_recv()
    earlier = jnp.where(s > 0, halo[...].astype(F32), 0.0)
    sequence = jnp.concatenate([earlier, feats], 0)
    conv = jnp.zeros(dec.shape, F32)
    for tap in range(3):
        begin = (2 - tap) * SPOTS
        window = sequence[begin : begin + TOK_DEV].astype(BF16)
        conv = conv + jnp.dot(window, taps[tap], preferred_element_type=F32)
    dec[...] = (conv / (1.0 + jnp.exp(-conv))).astype(BF16)
    post.drain()
    assert len(post.copies) == COPIES


def layer(levels, visible, counts, lat, mod, wqkv, gain, wout, whead, conv_w):
    rows, width, depth = 16 * TOK_DEV, lat.shape[1], wout.shape[0]
    vmem = pl.BlockSpec(memory_space=pltpu.VMEM)
    smem = pl.BlockSpec(memory_space=pltpu.SMEM)
    hbm = pl.BlockSpec(memory_space=pltpu.HBM)
    block = pltpu.VMEM((TOK_DEV, width), BF16)
    edge = pltpu.VMEM((2 * SPOTS, 128), BF16)
    return pl.pallas_call(
        layer_kernel,
        out_shape=(
            jax.ShapeDtypeStruct(lat.shape, BF16),
            jax.ShapeDtypeStruct((lat.shape[0], conv_w.shape[2]), BF16),
        ),
        in_specs=[smem, smem, smem] + [hbm] * 7,
        out_specs=(vmem, vmem),
        scratch_shapes=[
            block,
            pltpu.VMEM(mod.shape, F32),
            pltpu.VMEM(gain.shape, F32),
            pltpu.VMEM((rows, width), BF16),
            pltpu.VMEM((3, width, WIDE), BF16),
            pltpu.VMEM((rows, WIDE), BF16),
            pltpu.VMEM((rows, WIDE), BF16),
            pltpu.VMEM((rows, WIDE), BF16),
            pltpu.VMEM((8, KEEP, 128, 2 * WIDE), BF16),
            pltpu.VMEM((2, rows, 1), F32),
            pltpu.VMEM((2, rows, 1), F32),
            pltpu.VMEM((2, rows, HD), F32),
            pltpu.VMEM((8, 2, TOK_DEV, WIDE), BF16),
            pltpu.VMEM((8, TOK_DEV, WIDE), BF16),
            pltpu.VMEM((2 * depth, width), BF16),
            pltpu.VMEM((8, TOK_DEV, width), F32),
            pltpu.VMEM((8, TOK_DEV, width), BF16),
            block, block, block, block, block, block, block,
            pltpu.VMEM((128, width), BF16),
            pltpu.VMEM((3, 128, conv_w.shape[2]), BF16),
            edge,
            edge,
            pltpu.SemaphoreType.DMA((COPIES,)),
            pltpu.SemaphoreType.DMA((COPIES,)),
            pltpu.SemaphoreType.DMA((9,)),
        ],
        compiler_params=pltpu.CompilerParams(
            collective_id=0, has_side_effects=True, vmem_limit_bytes=58 * 2**20
        ),
        name="layer",
    )(levels, visible, counts, lat, mod, wqkv, gain, wout, whead, conv_w)


def per_device(
    latents, levels, visible, frame_counts, modulation, w_qkv, qk_gain, w_out, w_head, conv_w
):
    denoised, decoded = layer(
        levels, visible, frame_counts, latents[0], modulation.transpose(1, 0, 2),
        w_qkv.transpose(1, 0, 2), qk_gain, w_out, w_head.T, conv_w,
    )
    return (denoised[None], decoded[None])


def solution(mesh):
    placed = (
        P("span", "tok", None),
        P("span"),
        P(),
        P(),
        P(),
        P(None, None, "tok"),
        P(None, "tok"),
        P("tok", None),
        P(),
        P(),
    )
    return jax.shard_map(
        per_device,
        mesh=mesh,
        in_specs=placed,
        out_specs=(P("span", "tok", None), P("span", "tok", None)),
        check_vma=False,
    )
```

```python
import jax
import jax.numpy as jnp
from jax import lax
from jax.experimental import pallas as pl
from jax.experimental.pallas import tpu as pltpu
from jax.sharding import PartitionSpec as P

HD = 128
FRAMES = 8
KEEP = 2
SPOTS = 8
TOK_DEV = 64
EPS = 1e-06
LOG2E = 1.4426950408889634

MESH = pl.DeviceIdType.MESH
F32 = jnp.float32
BF16 = jnp.bfloat16

OWN, DOWN, UP, FAR, ACROSS, XDOWN, XUP, XFAR = range(8)
HALF = TOK_DEV // 2


def places():
    s = lax.axis_index("span")
    t = lax.axis_index("tok")
    z, yh, c = t // 4, (t // 2) % 2, t % 2
    x, yl = s // 2, s % 2

    def tok(z, yh, c):
        return z * 4 + yh * 2 + c

    return dict(
        s=s,
        up=(s, tok((z + 1) % 4, yh, c)),
        down=(s, tok((z + 3) % 4, yh, c)),
        across=(s, tok(z, 1 - yh, c)),
        twin=(s, tok(z, yh, 1 - c)),
        right=(((x + 1) % 4) * 2 + yl, t),
        left=(((x + 3) % 4) * 2 + yl, t),
        pair=(x * 2 + 1 - yl, t),
        after=((s + 1) % 8, t),
        before=((s + 7) % 8, t),
    )


def greet(at, names):
    barrier = pltpu.get_barrier_semaphore()
    for name in names:
        pl.semaphore_signal(barrier, inc=1, device_id=at[name], device_id_type=MESH)
    return lambda: pl.semaphore_wait(barrier, len(names))


class Post:
    def __init__(self, send, recv):
        self.send, self.recv, self.copies = send, recv, []

    def __call__(self, src, dst, device):
        index = len(self.copies)
        copy = pltpu.make_async_remote_copy(
            src_ref=src,
            dst_ref=dst,
            send_sem=self.send.at[index],
            recv_sem=self.recv.at[index],
            device_id=device,
            device_id_type=MESH,
        )
        copy.start()
        self.copies.append(copy)
        return copy

    def drain(self):
        for copy in self.copies:
            copy.wait_send()

COPIES = 60 + 14 + 1 + 8 + 14 + 1
LEAD = KEEP * SPOTS
REST = TOK_DEV - LEAD
PENALTY = 1e30
WIDE = 2 * HD


def layer_kernel(
    levels, visible, counts, lat_in, mod_in, wqkv, gain_in, wout, whead,
    den, seq,
    lat, mod, gain, xlead, xrest, wbuf, qbuf, kbuf, vbuf, kvbuf, best, total, acc, att, atwin,
    obuf, partial, outbox, fx, cx, fo, yx, zd, zu, ya, heads, tail, halo,
    send, recv, local,
):
    at = places()
    s = at["s"]
    peers = ("twin", "up", "down", "across", "right", "left", "pair", "after", "before")
    met = greet(at, peers)
    width, depth = lat.shape[1], wout.shape[0]

    def load(index, source, target):
        copy = pltpu.make_async_copy(source, target, local.at[index])
        copy.start()
        return copy

    first_loads = [load(0, lat_in, lat), load(1, mod_in, mod), load(2, gain_in, gain)]
    weights = [load(3 + j, wqkv.at[j], wbuf.at[j]) for j in range(3)]
    late_loads = [
        load(6, wout, obuf.at[pl.ds(0, depth)]),
        load(7, whead, heads.at[pl.ds(0, 96)]),
    ]
    for item in first_loads:
        item.wait()
    level = levels[0]
    shift = mod[0, pl.ds(level, 1), :]
    scale = 1.0 + mod[1, pl.ds(level, 1), :]

    def modulate(row, target, place):
        values = lat[row : row + LEAD, :].astype(F32)
        centre = values - jnp.mean(values, -1, keepdims=True)
        spread = jnp.mean(centre * centre, -1, keepdims=True)
        target[place : place + LEAD, :] = (
            centre * lax.rsqrt(spread + EPS) * scale + shift
        ).astype(BF16)

    modulate(0, xlead, 0)
    met()
    post = Post(send, recv)

    class Gather:
        def __init__(self, buffer, rows):
            self.buffer, self.rows = buffer, rows
            self.twin, self.up, self.down, self.across = {}, {}, {}, {}
            self.far, self.over, self.cross_y, self.over_far = {}, {}, {}, {}

        def part(self, place, core, half):
            return self.buffer.at[
                pl.ds((place * 2 + core) * self.rows, self.rows),
                pl.ds(half * (width // 2), width // 2),
            ]

        def hand(self, place, half):
            self.twin[place, half] = post(
                self.part(place, 0, half), self.part(place, 1, half), at["twin"]
            )

        def move(self, source, target, half, to):
            return post(self.part(source, 0, half), self.part(target, 0, half), at[to])

        def settle(self, *names):
            for place in names:
                for half in range(2):
                    self.twin[place, half].wait_recv()

        def begin(self):
            for first in (0, 1):
                self.up[first] = self.move(OWN, DOWN, first, "up")
                self.down[1 - first] = self.move(OWN, UP, 1 - first, "down")
                self.across[first] = self.move(OWN, ACROSS, first, "across")
                self.hand(OWN, first)

        def near(self):
            self.up[0].wait_recv()
            self.far[0] = self.move(DOWN, FAR, 0, "up")
            self.cross_y[0] = self.move(DOWN, XDOWN, 0, "across")
            self.hand(DOWN, 0)
            self.down[1].wait_recv()
            self.far[1] = self.move(UP, FAR, 1, "down")
            self.cross_y[1] = self.move(UP, XUP, 1, "across")
            self.hand(UP, 1)
            self.across[0].wait_recv()
            self.over[0] = self.move(ACROSS, XUP, 0, "down")
            self.hand(ACROSS, 0)
            self.across[1].wait_recv()
            self.over[1] = self.move(ACROSS, XDOWN, 1, "up")
            self.hand(ACROSS, 1)
            self.up[1].wait_recv()
            self.hand(DOWN, 1)
            self.down[0].wait_recv()
            self.hand(UP, 0)

        def turn(self, half):
            self.cross_y[half].wait_recv()
            source, to = ((XDOWN, "up"), (XUP, "down"))[half]
            self.over_far[half] = self.move(source, XFAR, half, to)
            self.hand(source, half)

        def opposite(self):
            for half in range(2):
                self.far[half].wait_recv()
                self.hand(FAR, half)

        def beside(self):
            self.over[1].wait_recv()
            self.hand(XDOWN, 1)
            self.over[0].wait_recv()
            self.hand(XUP, 0)

        def last(self):
            for half in range(2):
                self.over_far[half].wait_recv()
                self.hand(XFAR, half)

    early = Gather(xlead, LEAD)
    later = Gather(xrest, REST)
    early.begin()
    for row in range(LEAD, TOK_DEV, LEAD):
        modulate(row, xrest, row - LEAD)

    def project(slot, tiles, lead):
        rows = LEAD if lead else REST
        x = (xlead if lead else xrest)[slot * rows : (slot + tiles) * rows, :]
        for j, out in enumerate((qbuf, kbuf, vbuf)):
            p = jnp.dot(x, wbuf[j], preferred_element_type=F32)
            if j < 2:
                parts = []
                for h in range(2):
                    t = p[:, h * HD : (h + 1) * HD]
                    square = jnp.mean(t * t, -1, keepdims=True)
                    g = gain[j : j + 1, h * HD : (h + 1) * HD]
                    if j == 0:
                        g = g * (LOG2E * HD ** (-0.5))
                    parts.append(t * lax.rsqrt(square + EPS) * g)
                p = jnp.concatenate(parts, -1)
            first = 0 if lead else LEAD
            out[slot : slot + tiles, first : first + rows, :] = p.reshape(
                tiles, rows, WIDE
            ).astype(BF16)
            if j > 0 and lead:
                frames = p.reshape(tiles, KEEP, SPOTS, WIDE)
                for f in range(KEEP):
                    kvbuf[0, f, :, (j - 1) * WIDE : j * WIDE] = (
                        frames[:, f].reshape(tiles * SPOTS, WIDE).astype(BF16)
                    )

    def spread(source, target, f, to):
        return post(kvbuf.at[source, f], kvbuf.at[target, f], at[to])

    early.near()
    early.turn(0)
    early.turn(1)
    later.begin()
    wtwin = post(wout, obuf.at[pl.ds(depth, depth)], at["twin"])
    early.opposite()
    early.beside()
    early.last()
    for item in weights:
        item.wait()
    early.settle(*range(8))
    project(0, 16, True)
    right = [spread(0, 1, f, "right") for f in (0, 1)]
    left = [spread(0, 3, f, "left") for f in (1, 0)][::-1]
    later.near()
    pair = [spread(0, 4, f, "pair") for f in (0, 1)]
    later.settle(OWN)
    project(0, 2, False)
    later.settle(DOWN, UP)
    right[0].wait_recv()
    far = [spread(1, 2, 0, "right")]
    left[1].wait_recv()
    far.append(spread(3, 2, 1, "left"))
    project(2, 4, False)
    later.turn(0)
    later.opposite()
    later.settle(FAR, ACROSS)
    later.turn(1)
    project(6, 4, False)
    later.beside()
    over_right, over_left = {}, {}

    def cross(f):
        pair[f].wait_recv()
        over_right[f] = spread(4, 5, f, "right")
        over_left[f] = spread(4, 7, f, "left")

    cross(0)
    later.settle(XDOWN, XUP)
    project(10, 4, False)
    cross(1)
    later.last()
    over_right[0].wait_recv()
    far.append(spread(5, 6, 0, "right"))
    later.settle(XFAR)
    project(14, 2, False)
    over_left[1].wait_recv()
    far.append(spread(7, 6, 1, "left"))

    contract = (((1,), (1,)), ((), ()))
    x, yl = s // 2, s % 2
    penalties = []
    for place in range(1, 8):
        source = ((x + 4 - place % 4) % 4) * 2 + (yl + place // 4) % 2
        seen = (source < s) & (visible[s, source] == 1)
        count = counts[source]
        penalties.append(
            [jnp.where(seen & (f < count), 0.0, PENALTY).astype(F32) for f in range(KEEP)]
        )

    def queries(place):
        return pl.ds(place * 128, 128)

    def tiles_of(place, cols):
        return qbuf[pl.ds(2 * place, 2), :, cols].reshape(128, HD)

    def own_clip(place):
        rows = queries(place)
        for h in range(2):
            cols = slice(h * HD, (h + 1) * HD)
            scores = lax.dot_general(
                tiles_of(place, cols), kbuf[:, :, cols].reshape(16 * TOK_DEV, HD), contract,
                preferred_element_type=F32,
            )
            top = jnp.max(scores, -1, keepdims=True)
            terms = jnp.exp2(scores - top)
            best[h, rows] = top
            total[h, rows] = jnp.sum(terms, -1, keepdims=True)
            acc[h, rows] = jnp.dot(
                terms.astype(BF16), vbuf[:, :, cols].reshape(16 * TOK_DEV, HD),
                preferred_element_type=F32,
            )

    def earlier_clips(place):
        rows = queries(place)
        for h in range(2):
            cols = slice(h * HD, (h + 1) * HD)
            query = tiles_of(place, cols)
            old = best[h, rows]
            top = old
            scores = []
            for i in range(7):
                for f in range(KEEP):
                    piece = lax.dot_general(
                        query, kvbuf[i + 1, f, :, cols], contract, preferred_element_type=F32
                    )
                    scores.append(piece)
                    top = jnp.maximum(
                        top, jnp.max(piece, -1, keepdims=True) - penalties[i][f]
                    )
            decay = jnp.exp2(old - top)
            terms = [
                jnp.exp2(piece - (top + penalties[n // 2][n % 2]))
                for n, piece in enumerate(scores)
            ]
            plain = terms[0]
            for term in terms[1:]:
                plain = plain + term
            norm = total[h, rows] * decay + jnp.sum(plain, -1, keepdims=True)
            values = kvbuf[1:8, :, :, WIDE + h * HD : WIDE + (h + 1) * HD].reshape(7 * WIDE, HD)
            mixed = acc[h, rows] * decay + jnp.dot(
                jnp.concatenate([term.astype(BF16) for term in terms], -1),
                values,
                preferred_element_type=F32,
            )
            out = (mixed / norm).astype(BF16)
            att[place, 0, :, cols] = out[:TOK_DEV]
            att[place, 1, :, cols] = out[TOK_DEV:]

    shared = {}

    def swap(place):
        shared[place] = post(att.at[place, 1], atwin.at[place], at["twin"])

    tile = 512

    def multiply(*spots):
        for p in spots:
            shared[p].wait_recv()
        a = jnp.concatenate(
            [jnp.concatenate([att[p, 0], atwin[p]], -1) for p in spots], 0
        )
        for col in range(0, width, tile):
            r = jnp.dot(a, obuf[:, col : col + tile], preferred_element_type=F32)
            for i, p in enumerate(spots):
                partial[p, :, col : col + tile] = r[i * TOK_DEV : (i + 1) * TOK_DEV]

    def ship(spot, half, box, to, *added):
        rows = slice(half * HALF, (half + 1) * HALF)
        value = partial[spot, rows, :]
        for other in added:
            value = value + other[rows, :].astype(F32)
        outbox[spot, rows, :] = value.astype(BF16)
        piece = pl.ds(half * HALF, HALF)
        return post(outbox.at[spot, piece], box.at[piece], at[to])

    own_clip(XFAR)
    own_clip(XDOWN)
    own_clip(XUP)
    for copy in (right[1], left[0], over_right[1], over_left[0], *far):
        copy.wait_recv()
    earlier_clips(XFAR)
    swap(XFAR)
    for item in late_loads:
        item.wait()
    wtwin.wait_recv()
    heads[96:, :] = jnp.zeros((32, width), BF16)
    multiply(XFAR)
    fx0 = ship(XFAR, 0, fx, "up")
    fx1 = ship(XFAR, 1, fx, "down")

    earlier_clips(XDOWN)
    swap(XDOWN)
    earlier_clips(XUP)
    swap(XUP)
    own_clip(FAR)
    multiply(XDOWN, XUP)
    cx1 = ship(XUP, 1, cx, "up")
    cx0 = ship(XDOWN, 0, cx, "down")
    earlier_clips(FAR)
    swap(FAR)
    fx0.wait_recv()
    yx0 = ship(XUP, 0, yx, "across", fx)
    fx1.wait_recv()
    yx1 = ship(XDOWN, 1, yx, "across", fx)
    multiply(FAR)
    fo0 = ship(FAR, 0, fo, "up")
    fo1 = ship(FAR, 1, fo, "down")

    def rest(index, carry):
        own_clip(index)
        earlier_clips(index)
        return carry

    lax.fori_loop(DOWN, UP + 1, rest, 0)
    swap(DOWN)
    swap(UP)
    own_clip(ACROSS)
    multiply(DOWN, UP)
    zd1 = ship(UP, 1, zd, "up")
    zu0 = ship(DOWN, 0, zu, "down")
    earlier_clips(ACROSS)
    swap(ACROSS)
    own_clip(OWN)
    multiply(ACROSS)
    cx1.wait_recv()
    ya1 = ship(ACROSS, 1, ya, "across", cx)
    cx0.wait_recv()
    ya0 = ship(ACROSS, 0, ya, "across", cx)
    fo0.wait_recv()
    yx0.wait_recv()
    zd0 = ship(UP, 0, zd, "up", fo, yx)
    fo1.wait_recv()
    yx1.wait_recv()
    zu1 = ship(DOWN, 1, zu, "down", fo, yx)
    earlier_clips(OWN)
    swap(OWN)
    multiply(OWN)

    gate = mod[2, pl.ds(level, 1), :]
    for copy in (zd1, zu0, ya1, zd0, zu1, ya0):
        copy.wait_recv()
    for row in range(0, TOK_DEV, 16):
        piece = slice(row, row + 16)
        mixed = partial[OWN, piece, :]
        for box in (zd, zu, ya):
            mixed = mixed + box[piece, :].astype(F32)
        den[piece, :] = (lat[piece, :].astype(F32) + gate * mixed).astype(BF16)
    feats = lax.dot_general(
        den[...], heads[...], contract, preferred_element_type=F32
    ).astype(BF16).astype(F32)
    tail[...] = feats[TOK_DEV - 2 * SPOTS :].astype(BF16)
    edge = post(tail, halo, at["after"])
    edge.wait_recv()
    earlier = jnp.where(s > 0, halo[...].astype(F32), 0.0)
    seq[: 2 * SPOTS, :] = earlier.astype(BF16)
    seq[2 * SPOTS :, :] = feats.astype(BF16)
    post.drain()
    assert len(post.copies) == COPIES


def decode_kernel(den_in, seq, conv_w, den, dec, taps):
    den[...] = den_in[...]
    taps[:, 96:, :] = jnp.zeros((3, 32, taps.shape[2]), BF16)
    taps[:, :96, :] = conv_w[...]
    sequence = seq[...].astype(F32)
    conv = jnp.zeros(dec.shape, F32)
    for tap in range(3):
        begin = (2 - tap) * SPOTS
        window = sequence[begin : begin + TOK_DEV].astype(BF16)
        conv = conv + jnp.dot(window, taps[tap], preferred_element_type=F32)
    dec[...] = (conv / (1.0 + jnp.exp(-conv))).astype(BF16)


def decode(den, seq, conv_w):
    vmem = pl.BlockSpec(memory_space=pltpu.VMEM)
    return pl.pallas_call(
        decode_kernel,
        out_shape=(
            jax.ShapeDtypeStruct(den.shape, BF16),
            jax.ShapeDtypeStruct((den.shape[0], conv_w.shape[2]), BF16),
        ),
        in_specs=[vmem] * 3,
        out_specs=(vmem, vmem),
        scratch_shapes=[pltpu.VMEM((3, 128, conv_w.shape[2]), BF16)],
        compiler_params=pltpu.CompilerParams(vmem_limit_bytes=58 * 2**20),
        name="decode",
    )(den, seq, conv_w)


def layer(levels, visible, counts, lat, mod, wqkv, gain, wout, whead):
    rows, width, depth = 16 * TOK_DEV, lat.shape[1], wout.shape[0]
    vmem = pl.BlockSpec(memory_space=pltpu.VMEM)
    smem = pl.BlockSpec(memory_space=pltpu.SMEM)
    hbm = pl.BlockSpec(memory_space=pltpu.HBM)
    block = pltpu.VMEM((TOK_DEV, width), BF16)
    edge = pltpu.VMEM((2 * SPOTS, 128), BF16)
    return pl.pallas_call(
        layer_kernel,
        out_shape=(
            jax.ShapeDtypeStruct(lat.shape, BF16),
            jax.ShapeDtypeStruct((lat.shape[0] + 2 * SPOTS, 128), BF16),
        ),
        in_specs=[smem, smem, smem] + [hbm] * 6,
        out_specs=(vmem, vmem),
        scratch_shapes=[
            block,
            pltpu.VMEM(mod.shape, F32),
            pltpu.VMEM(gain.shape, F32),
            pltpu.VMEM((16 * LEAD, width), BF16),
            pltpu.VMEM((16 * REST, width), BF16),
            pltpu.VMEM((3, width, WIDE), BF16),
            pltpu.VMEM((16, TOK_DEV, WIDE), BF16),
            pltpu.VMEM((16, TOK_DEV, WIDE), BF16),
            pltpu.VMEM((16, TOK_DEV, WIDE), BF16),
            pltpu.VMEM((8, KEEP, 128, 2 * WIDE), BF16),
            pltpu.VMEM((2, rows, 1), F32),
            pltpu.VMEM((2, rows, 1), F32),
            pltpu.VMEM((2, rows, HD), F32),
            pltpu.VMEM((8, 2, TOK_DEV, WIDE), BF16),
            pltpu.VMEM((8, TOK_DEV, WIDE), BF16),
            pltpu.VMEM((2 * depth, width), BF16),
            pltpu.VMEM((8, TOK_DEV, width), F32),
            pltpu.VMEM((8, TOK_DEV, width), BF16),
            block, block, block, block, block, block, block,
            pltpu.VMEM((128, width), BF16),
            edge,
            edge,
            pltpu.SemaphoreType.DMA((COPIES,)),
            pltpu.SemaphoreType.DMA((COPIES,)),
            pltpu.SemaphoreType.DMA((8,)),
        ],
        compiler_params=pltpu.CompilerParams(
            collective_id=0, has_side_effects=True, vmem_limit_bytes=58 * 2**20
        ),
        name="layer",
    )(levels, visible, counts, lat, mod, wqkv, gain, wout, whead)


def per_device(
    latents, levels, visible, frame_counts, modulation, w_qkv, qk_gain, w_out, w_head, conv_w
):
    denoised, sequence = layer(
        levels, visible, frame_counts, latents[0], modulation.transpose(1, 0, 2),
        w_qkv.transpose(1, 0, 2), qk_gain, w_out, w_head.T,
    )
    denoised, decoded = decode(denoised, sequence, conv_w)
    return (denoised[None], decoded[None])


def solution(mesh):
    placed = (
        P("span", "tok", None),
        P("span"),
        P(),
        P(),
        P(),
        P(None, None, "tok"),
        P(None, "tok"),
        P("tok", None),
        P(),
        P(),
    )
    return jax.shard_map(
        per_device,
        mesh=mesh,
        in_specs=placed,
        out_specs=(P("span", "tok", None), P("span", "tok", None)),
        check_vma=False,
    )
```

```python
import jax
import jax.numpy as jnp
from jax import lax
from jax.experimental import pallas as pl
from jax.experimental.pallas import tpu as pltpu
from jax.sharding import PartitionSpec as P

HD = 128
FRAMES = 8
KEEP = 2
SPOTS = 8
TOK_DEV = 64
EPS = 1e-06
LOG2E = 1.4426950408889634

MESH = pl.DeviceIdType.MESH
F32 = jnp.float32
BF16 = jnp.bfloat16

OWN, DOWN, UP, FAR, ACROSS, XDOWN, XUP, XFAR = range(8)
HALF = TOK_DEV // 2


def places():
    s = lax.axis_index("span")
    t = lax.axis_index("tok")
    z, yh, c = t // 4, (t // 2) % 2, t % 2
    x, yl = s // 2, s % 2

    def tok(z, yh, c):
        return z * 4 + yh * 2 + c

    return dict(
        s=s,
        up=(s, tok((z + 1) % 4, yh, c)),
        down=(s, tok((z + 3) % 4, yh, c)),
        across=(s, tok(z, 1 - yh, c)),
        twin=(s, tok(z, yh, 1 - c)),
        right=(((x + 1) % 4) * 2 + yl, t),
        left=(((x + 3) % 4) * 2 + yl, t),
        pair=(x * 2 + 1 - yl, t),
        after=((s + 1) % 8, t),
        before=((s + 7) % 8, t),
    )


def greet(at, names):
    barrier = pltpu.get_barrier_semaphore()
    for name in names:
        pl.semaphore_signal(barrier, inc=1, device_id=at[name], device_id_type=MESH)
    return lambda: pl.semaphore_wait(barrier, len(names))


class Post:
    def __init__(self, send, recv):
        self.send, self.recv, self.copies = send, recv, []

    def __call__(self, src, dst, device):
        index = len(self.copies)
        copy = pltpu.make_async_remote_copy(
            src_ref=src,
            dst_ref=dst,
            send_sem=self.send.at[index],
            recv_sem=self.recv.at[index],
            device_id=device,
            device_id_type=MESH,
        )
        copy.start()
        self.copies.append(copy)
        return copy

    def drain(self):
        for copy in self.copies:
            copy.wait_send()

COPIES = 60 + 14 + 1 + 8 + 14 + 1
LEAD = KEEP * SPOTS
REST = TOK_DEV - LEAD
PENALTY = 1e30
WIDE = 2 * HD


def layer_kernel(
    levels, visible, counts, lat_in, mod_in, wqkv, gain_in, wout, whead,
    den, seq,
    lat, mod, gain, xlead, xrest, wbuf, qbuf, kbuf, vbuf, kvbuf, best, total, acc, att, atwin,
    obuf, partial, outbox, fx, cx, fo, yx, zd, zu, ya, heads, tail, halo,
    send, recv, local,
):
    at = places()
    s = at["s"]
    peers = ("twin", "up", "down", "across", "right", "left", "pair", "after", "before")
    met = greet(at, peers)
    width, depth = lat.shape[1], wout.shape[0]

    def load(index, source, target):
        copy = pltpu.make_async_copy(source, target, local.at[index])
        copy.start()
        return copy

    first_loads = [load(0, lat_in, lat), load(1, mod_in, mod), load(2, gain_in, gain)]
    weights = [load(3 + j, wqkv.at[j], wbuf.at[j]) for j in range(3)]
    late_loads = [
        load(6, wout, obuf.at[pl.ds(0, depth)]),
        load(7, whead, heads.at[pl.ds(0, 96)]),
    ]
    for item in first_loads:
        item.wait()
    level = levels[0]
    shift = mod[0, pl.ds(level, 1), :]
    scale = 1.0 + mod[1, pl.ds(level, 1), :]

    def modulate(row, target, place):
        values = lat[row : row + LEAD, :].astype(F32)
        centre = values - jnp.mean(values, -1, keepdims=True)
        spread = jnp.mean(centre * centre, -1, keepdims=True)
        target[place : place + LEAD, :] = (
            centre * lax.rsqrt(spread + EPS) * scale + shift
        ).astype(BF16)

    modulate(0, xlead, 0)
    met()
    post = Post(send, recv)

    class Gather:
        def __init__(self, buffer, rows):
            self.buffer, self.rows = buffer, rows
            self.twin, self.up, self.down, self.across = {}, {}, {}, {}
            self.far, self.over, self.cross_y, self.over_far = {}, {}, {}, {}

        def part(self, place, core, half):
            return self.buffer.at[
                pl.ds((place * 2 + core) * self.rows, self.rows),
                pl.ds(half * (width // 2), width // 2),
            ]

        def hand(self, place, half):
            self.twin[place, half] = post(
                self.part(place, 0, half), self.part(place, 1, half), at["twin"]
            )

        def move(self, source, target, half, to):
            return post(self.part(source, 0, half), self.part(target, 0, half), at[to])

        def settle(self, *names):
            for place in names:
                for half in range(2):
                    self.twin[place, half].wait_recv()

        def begin(self):
            for first in (0, 1):
                self.up[first] = self.move(OWN, DOWN, first, "up")
                self.down[1 - first] = self.move(OWN, UP, 1 - first, "down")
                self.across[first] = self.move(OWN, ACROSS, first, "across")
                self.hand(OWN, first)

        def near(self):
            self.up[0].wait_recv()
            self.far[0] = self.move(DOWN, FAR, 0, "up")
            self.cross_y[0] = self.move(DOWN, XDOWN, 0, "across")
            self.hand(DOWN, 0)
            self.down[1].wait_recv()
            self.far[1] = self.move(UP, FAR, 1, "down")
            self.cross_y[1] = self.move(UP, XUP, 1, "across")
            self.hand(UP, 1)
            self.across[0].wait_recv()
            self.over[0] = self.move(ACROSS, XUP, 0, "down")
            self.hand(ACROSS, 0)
            self.across[1].wait_recv()
            self.over[1] = self.move(ACROSS, XDOWN, 1, "up")
            self.hand(ACROSS, 1)
            self.up[1].wait_recv()
            self.hand(DOWN, 1)
            self.down[0].wait_recv()
            self.hand(UP, 0)

        def turn(self, half):
            self.cross_y[half].wait_recv()
            source, to = ((XDOWN, "up"), (XUP, "down"))[half]
            self.over_far[half] = self.move(source, XFAR, half, to)
            self.hand(source, half)

        def opposite(self):
            for half in range(2):
                self.far[half].wait_recv()
                self.hand(FAR, half)

        def beside(self):
            self.over[1].wait_recv()
            self.hand(XDOWN, 1)
            self.over[0].wait_recv()
            self.hand(XUP, 0)

        def last(self):
            for half in range(2):
                self.over_far[half].wait_recv()
                self.hand(XFAR, half)

    early = Gather(xlead, LEAD)
    later = Gather(xrest, REST)
    early.begin()
    for row in range(LEAD, TOK_DEV, LEAD):
        modulate(row, xrest, row - LEAD)

    def project(slot, tiles, lead):
        rows = LEAD if lead else REST
        x = (xlead if lead else xrest)[slot * rows : (slot + tiles) * rows, :]
        for j, out in enumerate((qbuf, kbuf, vbuf)):
            p = jnp.dot(x, wbuf[j], preferred_element_type=F32)
            if j < 2:
                parts = []
                for h in range(2):
                    t = p[:, h * HD : (h + 1) * HD]
                    square = jnp.mean(t * t, -1, keepdims=True)
                    g = gain[j : j + 1, h * HD : (h + 1) * HD]
                    if j == 0:
                        g = g * (LOG2E * HD ** (-0.5))
                    parts.append(t * lax.rsqrt(square + EPS) * g)
                p = jnp.concatenate(parts, -1)
            first = 0 if lead else LEAD
            out[slot : slot + tiles, first : first + rows, :] = p.reshape(
                tiles, rows, WIDE
            ).astype(BF16)
            if j > 0 and lead:
                frames = p.reshape(tiles, KEEP, SPOTS, WIDE)
                for f in range(KEEP):
                    kvbuf[0, f, :, (j - 1) * WIDE : j * WIDE] = (
                        frames[:, f].reshape(tiles * SPOTS, WIDE).astype(BF16)
                    )

    def spread(source, target, f, to):
        return post(kvbuf.at[source, f], kvbuf.at[target, f], at[to])

    early.near()
    early.turn(0)
    early.turn(1)
    later.begin()
    wtwin = post(wout, obuf.at[pl.ds(depth, depth)], at["twin"])
    early.opposite()
    early.beside()
    early.last()
    for item in weights:
        item.wait()
    early.settle(*range(8))
    project(0, 16, True)
    right = [spread(0, 1, f, "right") for f in (0, 1)]
    left = [spread(0, 3, f, "left") for f in (1, 0)][::-1]
    later.near()
    pair = [spread(0, 4, f, "pair") for f in (0, 1)]
    later.settle(OWN)
    project(0, 2, False)
    later.settle(DOWN, UP)
    right[0].wait_recv()
    far = [spread(1, 2, 0, "right")]
    left[1].wait_recv()
    far.append(spread(3, 2, 1, "left"))
    project(2, 4, False)
    later.turn(0)
    later.opposite()
    later.settle(FAR, ACROSS)
    later.turn(1)
    project(6, 4, False)
    later.beside()
    over_right, over_left = {}, {}

    def cross(f):
        pair[f].wait_recv()
        over_right[f] = spread(4, 5, f, "right")
        over_left[f] = spread(4, 7, f, "left")

    cross(0)
    later.settle(XDOWN, XUP)
    project(10, 4, False)
    cross(1)
    later.last()
    over_right[0].wait_recv()
    far.append(spread(5, 6, 0, "right"))
    later.settle(XFAR)
    project(14, 2, False)
    over_left[1].wait_recv()
    far.append(spread(7, 6, 1, "left"))

    contract = (((1,), (1,)), ((), ()))
    x, yl = s // 2, s % 2
    penalties = []
    for place in range(1, 8):
        source = ((x + 4 - place % 4) % 4) * 2 + (yl + place // 4) % 2
        seen = (source < s) & (visible[s, source] == 1)
        count = counts[source]
        penalties.append(
            [jnp.where(seen & (f < count), 0.0, PENALTY).astype(F32) for f in range(KEEP)]
        )

    def queries(place, count):
        return pl.ds(place * 128, count * 128)

    def tiles_of(place, count, cols):
        return qbuf[pl.ds(2 * place, 2 * count), :, cols].reshape(128 * count, HD)

    def own_clip(place, count=1):
        rows = queries(place, count)
        for h in range(2):
            cols = slice(h * HD, (h + 1) * HD)
            scores = lax.dot_general(
                tiles_of(place, count, cols), kbuf[:, :, cols].reshape(16 * TOK_DEV, HD), contract,
                preferred_element_type=F32,
            )
            top = jnp.max(scores, -1, keepdims=True)
            terms = jnp.exp2(scores - top)
            best[h, rows] = top
            total[h, rows] = jnp.sum(terms, -1, keepdims=True)
            acc[h, rows] = jnp.dot(
                terms.astype(BF16), vbuf[:, :, cols].reshape(16 * TOK_DEV, HD),
                preferred_element_type=F32,
            )

    def earlier_clips(place, count=1):
        rows = queries(place, count)
        for h in range(2):
            cols = slice(h * HD, (h + 1) * HD)
            query = tiles_of(place, count, cols)
            old = best[h, rows]
            scores = []
            for i in range(7):
                for f in range(KEEP):
                    piece = lax.dot_general(
                        query, kvbuf[i + 1, f, :, cols], contract, preferred_element_type=F32
                    )
                    scores.append(piece - penalties[i][f])
            peak = scores[0]
            for score in scores[1:]:
                peak = jnp.maximum(peak, score)
            top = jnp.maximum(old, jnp.max(peak, -1, keepdims=True))
            decay = jnp.exp2(old - top)
            terms = [jnp.exp2(score - top) for score in scores]
            plain = terms[0]
            for term in terms[1:]:
                plain = plain + term
            norm = total[h, rows] * decay + jnp.sum(plain, -1, keepdims=True)
            values = kvbuf[1:8, :, :, WIDE + h * HD : WIDE + (h + 1) * HD].reshape(7 * WIDE, HD)
            mixed = acc[h, rows] * decay + jnp.dot(
                jnp.concatenate([term.astype(BF16) for term in terms], -1),
                values,
                preferred_element_type=F32,
            )
            out = (mixed / norm).astype(BF16)
            att[place : place + count, :, :, cols] = out.reshape(count, 2, TOK_DEV, HD)

    shared = {}

    def swap(place):
        shared[place] = post(att.at[place, 1], atwin.at[place], at["twin"])

    tile = 512

    def multiply(*spots):
        for p in spots:
            shared[p].wait_recv()
        a = jnp.concatenate(
            [jnp.concatenate([att[p, 0], atwin[p]], -1) for p in spots], 0
        )
        for col in range(0, width, tile):
            r = jnp.dot(a, obuf[:, col : col + tile], preferred_element_type=F32)
            for i, p in enumerate(spots):
                partial[p, :, col : col + tile] = r[i * TOK_DEV : (i + 1) * TOK_DEV]

    def ship(spot, half, box, to, *added):
        rows = slice(half * HALF, (half + 1) * HALF)
        value = partial[spot, rows, :]
        for other in added:
            value = value + other[rows, :].astype(F32)
        outbox[spot, rows, :] = value.astype(BF16)
        piece = pl.ds(half * HALF, HALF)
        return post(outbox.at[spot, piece], box.at[piece], at[to])

    own_clip(XFAR)
    own_clip(XDOWN, 2)
    for copy in (right[1], left[0], over_right[1], over_left[0], *far):
        copy.wait_recv()
    earlier_clips(XFAR)
    swap(XFAR)
    for item in late_loads:
        item.wait()
    wtwin.wait_recv()
    heads[96:, :] = jnp.zeros((32, width), BF16)
    multiply(XFAR)
    fx0 = ship(XFAR, 0, fx, "up")
    fx1 = ship(XFAR, 1, fx, "down")

    earlier_clips(XDOWN, 2)
    swap(XDOWN)
    swap(XUP)
    own_clip(FAR)
    multiply(XDOWN, XUP)
    cx1 = ship(XUP, 1, cx, "up")
    cx0 = ship(XDOWN, 0, cx, "down")
    earlier_clips(FAR)
    swap(FAR)
    fx0.wait_recv()
    yx0 = ship(XUP, 0, yx, "across", fx)
    fx1.wait_recv()
    yx1 = ship(XDOWN, 1, yx, "across", fx)
    multiply(FAR)
    fo0 = ship(FAR, 0, fo, "up")
    fo1 = ship(FAR, 1, fo, "down")

    own_clip(ACROSS)
    earlier_clips(ACROSS)
    swap(ACROSS)

    own_clip(DOWN, 2)
    earlier_clips(DOWN, 2)
    swap(DOWN)
    swap(UP)
    multiply(ACROSS)
    cx1.wait_recv()
    ya1 = ship(ACROSS, 1, ya, "across", cx)
    cx0.wait_recv()
    ya0 = ship(ACROSS, 0, ya, "across", cx)
    multiply(DOWN, UP)
    zd1 = ship(UP, 1, zd, "up")
    zu0 = ship(DOWN, 0, zu, "down")
    own_clip(OWN)
    fo0.wait_recv()
    yx0.wait_recv()
    zd0 = ship(UP, 0, zd, "up", fo, yx)
    fo1.wait_recv()
    yx1.wait_recv()
    zu1 = ship(DOWN, 1, zu, "down", fo, yx)
    earlier_clips(OWN)
    swap(OWN)
    multiply(OWN)

    gate = mod[2, pl.ds(level, 1), :]
    for copy in (zd1, zu0, ya1, zd0, zu1, ya0):
        copy.wait_recv()
    for row in range(0, TOK_DEV, 16):
        piece = slice(row, row + 16)
        mixed = partial[OWN, piece, :]
        for box in (zd, zu, ya):
            mixed = mixed + box[piece, :].astype(F32)
        den[piece, :] = (lat[piece, :].astype(F32) + gate * mixed).astype(BF16)
    feats = lax.dot_general(
        den[...], heads[...], contract, preferred_element_type=F32
    ).astype(BF16).astype(F32)
    tail[...] = feats[TOK_DEV - 2 * SPOTS :].astype(BF16)
    edge = post(tail, halo, at["after"])
    edge.wait_recv()
    earlier = jnp.where(s > 0, halo[...].astype(F32), 0.0)
    seq[: 2 * SPOTS, :] = earlier.astype(BF16)
    seq[2 * SPOTS :, :] = feats.astype(BF16)
    post.drain()
    assert len(post.copies) == COPIES


def decode_kernel(den_in, seq, conv_w, den, dec, taps):
    den[...] = den_in[...]
    taps[:, 96:, :] = jnp.zeros((3, 32, taps.shape[2]), BF16)
    taps[:, :96, :] = conv_w[...]
    sequence = seq[...].astype(F32)
    conv = jnp.zeros(dec.shape, F32)
    for tap in range(3):
        begin = (2 - tap) * SPOTS
        window = sequence[begin : begin + TOK_DEV].astype(BF16)
        conv = conv + jnp.dot(window, taps[tap], preferred_element_type=F32)
    dec[...] = (conv / (1.0 + jnp.exp(-conv))).astype(BF16)


def decode(den, seq, conv_w):
    vmem = pl.BlockSpec(memory_space=pltpu.VMEM)
    return pl.pallas_call(
        decode_kernel,
        out_shape=(
            jax.ShapeDtypeStruct(den.shape, BF16),
            jax.ShapeDtypeStruct((den.shape[0], conv_w.shape[2]), BF16),
        ),
        in_specs=[vmem] * 3,
        out_specs=(vmem, vmem),
        scratch_shapes=[pltpu.VMEM((3, 128, conv_w.shape[2]), BF16)],
        compiler_params=pltpu.CompilerParams(vmem_limit_bytes=58 * 2**20),
        name="decode",
    )(den, seq, conv_w)


def layer(levels, visible, counts, lat, mod, wqkv, gain, wout, whead):
    rows, width, depth = 16 * TOK_DEV, lat.shape[1], wout.shape[0]
    vmem = pl.BlockSpec(memory_space=pltpu.VMEM)
    smem = pl.BlockSpec(memory_space=pltpu.SMEM)
    hbm = pl.BlockSpec(memory_space=pltpu.HBM)
    block = pltpu.VMEM((TOK_DEV, width), BF16)
    edge = pltpu.VMEM((2 * SPOTS, 128), BF16)
    return pl.pallas_call(
        layer_kernel,
        out_shape=(
            jax.ShapeDtypeStruct(lat.shape, BF16),
            jax.ShapeDtypeStruct((lat.shape[0] + 2 * SPOTS, 128), BF16),
        ),
        in_specs=[smem, smem, smem] + [hbm] * 6,
        out_specs=(vmem, vmem),
        scratch_shapes=[
            block,
            pltpu.VMEM(mod.shape, F32),
            pltpu.VMEM(gain.shape, F32),
            pltpu.VMEM((16 * LEAD, width), BF16),
            pltpu.VMEM((16 * REST, width), BF16),
            pltpu.VMEM((3, width, WIDE), BF16),
            pltpu.VMEM((16, TOK_DEV, WIDE), BF16),
            pltpu.VMEM((16, TOK_DEV, WIDE), BF16),
            pltpu.VMEM((16, TOK_DEV, WIDE), BF16),
            pltpu.VMEM((8, KEEP, 128, 2 * WIDE), BF16),
            pltpu.VMEM((2, rows, 1), F32),
            pltpu.VMEM((2, rows, 1), F32),
            pltpu.VMEM((2, rows, HD), F32),
            pltpu.VMEM((8, 2, TOK_DEV, WIDE), BF16),
            pltpu.VMEM((8, TOK_DEV, WIDE), BF16),
            pltpu.VMEM((2 * depth, width), BF16),
            pltpu.VMEM((8, TOK_DEV, width), F32),
            pltpu.VMEM((8, TOK_DEV, width), BF16),
            block, block, block, block, block, block, block,
            pltpu.VMEM((128, width), BF16),
            edge,
            edge,
            pltpu.SemaphoreType.DMA((COPIES,)),
            pltpu.SemaphoreType.DMA((COPIES,)),
            pltpu.SemaphoreType.DMA((8,)),
        ],
        compiler_params=pltpu.CompilerParams(
            collective_id=0, has_side_effects=True, vmem_limit_bytes=58 * 2**20
        ),
        name="layer",
    )(levels, visible, counts, lat, mod, wqkv, gain, wout, whead)


def per_device(
    latents, levels, visible, frame_counts, modulation, w_qkv, qk_gain, w_out, w_head, conv_w
):
    denoised, sequence = layer(
        levels, visible, frame_counts, latents[0], modulation.transpose(1, 0, 2),
        w_qkv.transpose(1, 0, 2), qk_gain, w_out, w_head.T,
    )
    denoised, decoded = decode(denoised, sequence, conv_w)
    return (denoised[None], decoded[None])


def solution(mesh):
    placed = (
        P("span", "tok", None),
        P("span"),
        P(),
        P(),
        P(),
        P(None, None, "tok"),
        P(None, "tok"),
        P("tok", None),
        P(),
        P(),
    )
    return jax.shard_map(
        per_device,
        mesh=mesh,
        in_specs=placed,
        out_specs=(P("span", "tok", None), P("span", "tok", None)),
        check_vma=False,
    )
```
